32 devices in a mesh: imp: 8 (over z, y), camp: 4 (over x, core).
Axes of the slice: x: 2, y: 2, z: 4, core: 2. Of those that a mesh axis runs over, the one named last changes fastest.
Arguments:
- imp_emb: bfloat16 [16384, 256], P(('imp', 'camp')), may hold values from -512 to 512
- imp_cost: bfloat16 [16384], P(('imp', 'camp')), may hold values from 0.099609375 to 1
- camp_emb: bfloat16 [4096, 256], P(('camp', 'imp')), may hold values from -6 to 6
- prices: bfloat16 [4096], P(('camp', 'imp')), may hold values from -5 to 5
- spend_limits: float32 [4096], P(('camp', 'imp')), may hold values from 3 to 32
- block_lists: int32 [128, 4, 8], P('imp', 'camp'), may hold values from 0 to 7, as said below
- block_counts: int32 [128, 4], P('imp', 'camp'), may hold values from 1 to 8, as said below
Outputs:
- new_prices: float32 [4096], P(('camp', 'imp'))
- row_logz: float32 [16384], P('imp')
The draws below stay inside these ranges and needn't reach their ends.
Inputs may be any that keep to these rules, and one draw needn't show every extreme that they name: `block_lists`: entries of a list of one tile and owner are distinct block numbers of that owner; slots past the count hold block numbers too, which are ignored. `block_counts`: tile 0 uses all 8 slots of every owner.
All inputs are finite; a program needn't handle non-finite values.
Results may differ from the reference program's by a relative error of at most 0.0003.
Values may be sent and summed in bfloat16 or wider, within the bound.
A program may use at most 64 MiB of HBM per device.

```python
import math
import jax
import jax.numpy as jnp
from jax import lax

D = 256
BLOCK = 128
SLOTS = 8
TILES = 128
ROWS = 16384
OWN_BLOCKS = 8
CAMPAIGNS = 4096
N_CAMP = 4


def draw_imp_emb(key, part):
    base = jax.random.normal(jax.random.fold_in(key, 11), (ROWS, D), jnp.float32)
    base = jnp.clip(base, -6.0, 6.0)
    return base.astype(jnp.bfloat16)


def draw_block_lists(key, part):
    keys = jax.random.split(jax.random.fold_in(key, 23), TILES * N_CAMP)
    picks = jax.vmap(lambda one: jax.random.permutation(one, OWN_BLOCKS)[:SLOTS])(keys)
    return picks.reshape(TILES, N_CAMP, SLOTS).astype(jnp.int32)


def draw_block_counts(key, part):
    heavy = jax.random.randint(jax.random.fold_in(key, 31), (TILES, 1), SLOTS // 2, SLOTS + 1)
    spread = jax.random.randint(jax.random.fold_in(key, 37), (TILES, N_CAMP), 0, SLOTS)
    counts = 1 + spread * heavy // SLOTS
    counts = counts.at[0, :].set(SLOTS)
    return counts.astype(jnp.int32)


def block_levels(own_key, shape, cuts, low, largest):
    def one(dim, parts):
        steps = jax.random.uniform(jax.random.fold_in(jax.random.fold_in(own_key, 6), dim), (parts,), jnp.float32, low / len(cuts), largest / len(cuts))
        return jnp.repeat(jnp.exp(steps), shape[dim] // parts).reshape((-1,) + (1,) * (len(shape) - dim - 1))

    factor_of = one(*cuts[0])
    for cut in cuts[1:]:
        factor_of = factor_of * one(*cut)
    return factor_of


def scatter_about(stream_key, shape, deviation, reach, cuts=(), kind=jnp.bfloat16):
    values = jax.random.normal(stream_key, shape, jnp.float32) * deviation
    if len(cuts) > 0:
        values = block_levels(stream_key, shape, cuts, -0.22, 0.18) * values
    return jnp.clip(values, min=-reach, max=reach).astype(kind)


def setup_inputs(seed: int = 0) -> dict:
    streams_of = jax.random.split(jax.random.key(seed), 8)
    return {
        "imp_emb": draw_imp_emb(jax.random.fold_in(streams_of[7], 71), 0),
        "imp_cost": jnp.clip(jnp.exp(math.log(1.0) - 2.306499 * jax.random.uniform(streams_of[1], (ROWS,), jnp.float32) ** block_levels(streams_of[1], (ROWS,), ((0, 32),), -0.2, 0.2)), 0.099609375, 1.0).astype(jnp.bfloat16),
        "camp_emb": scatter_about(streams_of[2], (CAMPAIGNS, D), 1.0, 6.0, ((0, 32),)),
        "prices": scatter_about(streams_of[3], (CAMPAIGNS,), 1.0, 5.0, ((0, 32),)),
        "spend_limits": jnp.clip(jnp.exp(math.log(32.0) - 2.3671236 * jax.random.uniform(streams_of[4], (CAMPAIGNS,), jnp.float32) ** block_levels(streams_of[4], (CAMPAIGNS,), ((0, 32),), -0.2, 0.2)), 3.0, 32.0),
        "block_lists": draw_block_lists(jax.random.fold_in(streams_of[7], 71), 0),
        "block_counts": draw_block_counts(jax.random.fold_in(streams_of[7], 71), 0),
    }


def reference(imp_emb, imp_cost, camp_emb, prices, spend_limits, block_lists, block_counts):
    scale = 3.0 / jnp.sqrt(jnp.float32(D))
    camp_blocks = camp_emb.reshape(N_CAMP, OWN_BLOCKS, BLOCK, D)
    price_blocks = prices.astype(jnp.float32).reshape(N_CAMP, OWN_BLOCKS, BLOCK)
    tile_emb = imp_emb.reshape(TILES, BLOCK, D)
    tile_cost = imp_cost.astype(jnp.float32).reshape(TILES, BLOCK)
    owners = jnp.arange(N_CAMP, dtype=jnp.int32)[:, None]

    def per_tile(items):
        emb, cost, lists, counts = items
        chosen = camp_blocks[owners, lists].reshape(N_CAMP * SLOTS * BLOCK, D)
        chosen_price = price_blocks[owners, lists]
        raw = jnp.dot(emb, chosen.T, preferred_element_type=jnp.float32)
        logits = raw.reshape(BLOCK, N_CAMP, SLOTS, BLOCK) * scale - chosen_price[None]
        live = (jnp.arange(SLOTS, dtype=jnp.int32)[None, :] < counts[:, None])[None, :, :, None]
        top = lax.optimization_barrier(jnp.max(jnp.where(live, logits, -jnp.inf), axis=(1, 2, 3)))
        expo = jnp.exp(jnp.where(live, logits - top[:, None, None, None], -jnp.inf))
        total = lax.optimization_barrier(jnp.sum(expo, axis=(1, 2, 3)))
        weight = expo / total[:, None, None, None]
        contrib = lax.optimization_barrier(jnp.sum(weight * cost[:, None, None, None], axis=0))
        return (contrib, top + jnp.log(total))
    contribs, logz = lax.map(per_tile, (tile_emb, tile_cost, block_lists, block_counts))
    owner_idx = jnp.broadcast_to(jnp.arange(N_CAMP, dtype=jnp.int32)[None, :, None], block_lists.shape)
    spend = jnp.zeros((N_CAMP, OWN_BLOCKS, BLOCK), jnp.float32).at[owner_idx, block_lists].add(contribs)
    spend = spend.reshape(CAMPAIGNS)
    new_prices = prices.astype(jnp.float32) + 2.0 * (spend - spend_limits) / (spend + spend_limits)
    return (new_prices, logz.reshape(ROWS))
```

```python
import functools

import jax
import jax.numpy as jnp
from jax import lax
from jax.experimental import pallas as pl
from jax.experimental.pallas import tpu as pltpu
from jax.sharding import PartitionSpec as P

D = 256
BLOCK = 128
LANES = 128
STORE_LIMIT = 24 << 20
MESH = pl.DeviceIdType.MESH


def flip(index, bits, size):
    if size & (size - 1):
        return lax.rem(index + bits, size)
    out, bit = index, 1
    while bit < size:
        if bits & bit:
            out = out + bit * (1 - 2 * lax.rem(index // bit, 2))
        bit *= 2
    return out


def unflip(index, bits, size):
    if size & (size - 1):
        return lax.rem(index + size - bits, size)
    return flip(index, bits, size)


def kernel(
    sizes, emb_ref, cost_ref, camp_ref, price_ref, limit_ref, list_ref, count_ref,
    new_ref, logz_ref,
    e_buf, cost_buf, c_buf, price_buf, p_wide, x_buf, m_buf, s_buf, live_buf, f_buf,
    stat_send, stat_recv, spend_send, spend_recv,
    local_sem, e_send, e_fwd, e_recv, c_send, c_fwd, c_recv, cost_send, cost_recv,
    price_send, price_recv, stat_ssem, stat_rsem, spend_ssem, spend_rsem,
):
    n_imp, n_camp, n_y, chunk = sizes
    n_z, n_x = n_imp // n_y, n_camp // 2
    n_b = n_imp
    n_t = n_camp * chunk
    stored = x_buf.shape[0] == n_b
    me_i, me_c = lax.axis_index("imp"), lax.axis_index("camp")
    z, y = me_i // n_y, lax.rem(me_i, n_y)
    x, k = me_c // 2, lax.rem(me_c, 2)
    partner = 2 * x + (1 - k)
    scale = 3.0 / jnp.sqrt(jnp.float32(D))

    imp_peers = [
        flip(z, dz, n_z) * n_y + flip(y, dy, n_y)
        for dz in range(n_z) for dy in range(n_y) if dz or dy
    ]
    camp_peers = [partner] + [
        2 * flip(x, dx, n_x) + kk for dx in range(1, n_x) for kk in (k, 1 - k)
    ]

    own_copies = [
        pltpu.make_async_copy(camp_ref, c_buf.at[me_i], local_sem.at[0]),
        pltpu.make_async_copy(price_ref, price_buf.at[me_i], local_sem.at[1]),
        pltpu.make_async_copy(cost_ref, cost_buf.at[me_c], local_sem.at[2]),
        pltpu.make_async_copy(emb_ref, e_buf.at[pl.ds(me_c * chunk, chunk)], local_sem.at[3]),
    ]
    for copy in own_copies:
        copy.start()

    barrier = pltpu.get_barrier_semaphore()
    for peer in imp_peers:
        pl.semaphore_signal(barrier, inc=1, device_id={"imp": peer, "camp": me_c}, device_id_type=MESH)
    for peer in camp_peers:
        pl.semaphore_signal(barrier, inc=1, device_id={"imp": me_i, "camp": peer}, device_id_type=MESH)
    pl.semaphore_wait(barrier, len(imp_peers) + len(camp_peers))

    sends = []

    def send(src, dst, ssem, rsem, imp, camp):
        copy = pltpu.make_async_remote_copy(
            src_ref=src, dst_ref=dst, send_sem=ssem, recv_sem=rsem,
            device_id={"imp": imp, "camp": camp}, device_id_type=MESH,
        )
        copy.start()
        sends.append(copy)

    def arrived(dst, ssem, rsem):
        pltpu.make_async_remote_copy(
            src_ref=dst, dst_ref=dst, send_sem=ssem, recv_sem=rsem,
            device_id={"imp": me_i, "camp": partner}, device_id_type=MESH,
        ).wait_recv()

    for dy in range(1, n_y):
        send(camp_ref, c_buf.at[me_i], c_send.at[dy - 1], c_recv.at[me_i],
             z * n_y + flip(y, dy, n_y), me_c)
    for dz in range(1, n_z):
        send(camp_ref, c_buf.at[me_i], c_send.at[n_y - 1 + dz - 1], c_recv.at[me_i],
             flip(z, dz, n_z) * n_y + y, me_c)
    for t in range(chunk):
        for dx in range(1, n_x):
            send(emb_ref.at[t], e_buf.at[me_c * chunk + t], e_send.at[dx, t],
                 e_recv.at[me_c * chunk + t], me_i, 2 * flip(x, dx, n_x) + k)
        send(emb_ref.at[t], e_buf.at[me_c * chunk + t], e_send.at[0, t],
             e_recv.at[me_c * chunk + t], me_i, partner)
    for n, peer in enumerate(imp_peers):
        send(price_ref, price_buf.at[me_i], price_send.at[n], price_recv.at[me_i], peer, me_c)
    for n, peer in enumerate(camp_peers):
        send(cost_ref, cost_buf.at[me_c], cost_send.at[n], cost_recv.at[me_c], me_i, peer)

    slot = lax.broadcasted_iota(jnp.int32, list_ref.shape, 1)
    named = jnp.where(slot < count_ref[...], list_ref[...], -1)

    def mark(b, carry):
        hit = jnp.max(jnp.where(named == b, 1.0, 0.0), axis=1, keepdims=True)
        live_buf[b] = jnp.broadcast_to(hit, (n_t, LANES))
        return carry

    lax.fori_loop(0, n_b, mark, 0)

    for copy in own_copies:
        copy.wait()

    def widen(b):
        p_wide[b] = jnp.broadcast_to(price_buf[b], (BLOCK, LANES)).T

    def score(b, first, count):
        wide = e_buf[pl.ds(first, count)].reshape(count * BLOCK, D)
        raw = lax.dot_general(
            c_buf[b], wide, (((1,), (1,)), ((), ())), preferred_element_type=jnp.float32
        )
        return raw

    def both(b, first, count):
        raw = score(b, first, count)
        for t in range(count):
            logit = raw[:, t * LANES:(t + 1) * LANES] * scale - p_wide[b]
            top = jnp.max(logit, axis=0, keepdims=True)
            expo = jnp.exp(logit - top)
            m_buf[b, pl.ds(first + t, 1), :] = top
            s_buf[b, pl.ds(first + t, 1), :] = jnp.sum(expo, axis=0, keepdims=True)
            if stored:
                x_buf[b, first + t] = expo

    def near(b):
        def step(h, carry):
            both(b, 2 * x * chunk + h * chunk, chunk)
            return carry

        lax.fori_loop(0, 2, step, 0)

    def block_in(b):
        arrived(price_buf.at[b], price_send.at[0], price_recv.at[b])
        widen(b)

    def rows_in(dx, t):
        other = flip(x, dx, n_x)
        tile = (2 * other + k) * chunk + t
        arrived(e_buf.at[tile], e_send.at[0, 0], e_recv.at[tile])
        send(e_buf.at[tile], e_buf.at[tile], e_fwd.at[dx, t], e_recv.at[tile], me_i, partner)

    widen(me_i)
    for t in range(chunk):
        tile = partner * chunk + t
        arrived(e_buf.at[tile], e_send.at[0, 0], e_recv.at[tile])
    near(me_i)

    order = [(0, dy) for dy in range(1, n_y)] + [(dz, 0) for dz in range(1, n_z)]
    order += [(dz, dy) for dz in range(1, n_z) for dy in range(1, n_y)]
    chunks = [(dx, t) for t in range(chunk) for dx in range(1, n_x)]
    for n, (dz, dy) in enumerate(order):
        b = flip(z, dz, n_z) * n_y + flip(y, dy, n_y)
        arrived(c_buf.at[b], c_send.at[0], c_recv.at[b])
        if dy == 0:
            for fy in range(1, n_y):
                send(c_buf.at[b], c_buf.at[b], c_fwd.at[dz, fy], c_recv.at[b],
                     z * n_y + flip(y, fy, n_y), me_c)
        block_in(b)
        near(b)
        if chunks and n < len(order) - 1:
            rows_in(*chunks.pop(0))
    while chunks:
        rows_in(*chunks.pop(0))

    for dx in range(1, n_x):
        other = flip(x, dx, n_x)
        for t in range(chunk):
            tile = (2 * other + (1 - k)) * chunk + t
            arrived(e_buf.at[tile], e_send.at[0, 0], e_recv.at[tile])
        for kk in (k, 1 - k):
            def far(b, carry):
                both(b, (2 * other + kk) * chunk, chunk)
                return carry

            lax.fori_loop(0, n_b, far, 0)

    def block_top(b):
        return jnp.where(live_buf[b] > 0.0, m_buf[b], -jnp.inf)

    top_here = lax.fori_loop(
        0, n_b, lambda b, top: jnp.maximum(top, block_top(b)),
        jnp.full((n_t, LANES), -jnp.inf, jnp.float32),
    )
    total_here = lax.fori_loop(
        0, n_b, lambda b, total: total + s_buf[b] * jnp.exp(block_top(b) - top_here),
        jnp.zeros((n_t, LANES), jnp.float32),
    )
    stat_send[0] = top_here
    stat_send[1] = total_here
    for n, peer in enumerate(camp_peers):
        send(stat_send, stat_recv.at[me_c], stat_ssem.at[n], stat_rsem.at[me_c], me_i, peer)
    for peer in camp_peers:
        arrived(cost_buf.at[peer], cost_send.at[0], cost_recv.at[peer])
    cost = jnp.concatenate([cost_buf[g] for g in range(n_camp)], axis=0)
    stat_recv[me_c] = stat_send[...]
    for peer in camp_peers:
        arrived(stat_recv.at[peer], stat_ssem.at[0], stat_rsem.at[peer])
    top = stat_recv[0, 0]
    for g in range(1, n_camp):
        top = jnp.maximum(top, stat_recv[g, 0])
    total = jnp.zeros_like(top)
    for g in range(n_camp):
        total = total + stat_recv[g, 1] * jnp.exp(stat_recv[g, 0] - top)
    logz_ref[...] = top + jnp.log(total)
    ratio = cost / total

    def factor(b, carry):
        f_buf[b] = ratio * jnp.exp(block_top(b) - top)
        return carry

    lax.fori_loop(0, n_b, factor, 0)

    def spend_of(b):
        def step(h, acc):
            first = h * chunk
            if not stored:
                raw = score(b, first, chunk)
            for t in range(chunk):
                if stored:
                    expo = x_buf[b, first + t]
                else:
                    logit = raw[:, t * LANES:(t + 1) * LANES] * scale - p_wide[b]
                    expo = jnp.exp(logit - m_buf[b, pl.ds(first + t, 1), :])
                acc = acc + expo * f_buf[b, pl.ds(first + t, 1), :]
            return acc

        acc = lax.fori_loop(0, n_camp, step, jnp.zeros((BLOCK, LANES), jnp.float32))
        return jnp.sum(acc.T, axis=0, keepdims=True)

    for n, peer in enumerate(reversed(imp_peers)):
        spend_send[peer] = spend_of(peer)
        send(spend_send.at[peer], spend_recv.at[me_i], spend_ssem.at[n], spend_rsem.at[me_i],
             peer, me_c)
    mine = spend_of(me_i)
    for peer in imp_peers:
        arrived(spend_recv.at[peer], spend_ssem.at[0], spend_rsem.at[peer])
        mine = mine + spend_recv[peer]
    limit = limit_ref[...]
    new_ref[...] = price_buf[me_i] + 2.0 * (mine - limit) / (mine + limit)
    for copy in sends:
        copy.wait_send()


def local(n_y, imp_emb, imp_cost, camp_emb, prices, spend_limits, block_lists, block_counts):
    n_imp, n_camp = lax.axis_size("imp"), lax.axis_size("camp")
    chunk = imp_emb.shape[0] // BLOCK
    n_t = n_camp * chunk
    n_b = n_imp
    n_z = n_imp // n_y
    n_x = n_camp // 2
    f32, bf16 = jnp.float32, jnp.bfloat16
    stored = n_b * n_t * BLOCK * LANES * 4 <= STORE_LIMIT
    dma = pltpu.SemaphoreType.DMA
    anywhere, vmem = pl.BlockSpec(memory_space=pl.ANY), pl.BlockSpec(memory_space=pltpu.VMEM)
    new_prices, logz = pl.pallas_call(
        functools.partial(kernel, (n_imp, n_camp, n_y, chunk)),
        out_shape=(
            jax.ShapeDtypeStruct((1, LANES), f32),
            jax.ShapeDtypeStruct((n_t, LANES), f32),
        ),
        in_specs=[anywhere, anywhere, anywhere, anywhere, vmem, vmem, vmem],
        out_specs=(vmem, vmem),
        scratch_shapes=[
            pltpu.VMEM((n_t, BLOCK, D), bf16),
            pltpu.VMEM((n_camp, chunk, LANES), f32),
            pltpu.VMEM((n_b, BLOCK, D), bf16),
            pltpu.VMEM((n_b, 1, LANES), f32),
            pltpu.VMEM((n_b, BLOCK, LANES), f32),
            pltpu.VMEM((n_b, n_t, BLOCK, LANES) if stored else (1, 1, 8, LANES), f32),
            pltpu.VMEM((n_b, n_t, LANES), f32),
            pltpu.VMEM((n_b, n_t, LANES), f32),
            pltpu.VMEM((n_b, n_t, LANES), f32),
            pltpu.VMEM((n_b, n_t, LANES), f32),
            pltpu.VMEM((2, n_t, LANES), f32),
            pltpu.VMEM((n_camp, 2, n_t, LANES), f32),
            pltpu.VMEM((n_b, 1, LANES), f32),
            pltpu.VMEM((n_b, 1, LANES), f32),
            dma((4,)),
            dma((n_x, chunk)),
            dma((n_x, chunk)),
            dma((n_t,)),
            dma((n_y + n_z,)),
            dma((n_z, n_y)),
            dma((n_b,)),
            dma((n_camp,)),
            dma((n_camp,)),
            dma((n_imp,)),
            dma((n_imp,)),
            dma((n_camp,)),
            dma((n_camp,)),
            dma((n_imp,)),
            dma((n_imp,)),
        ],
        compiler_params=pltpu.CompilerParams(
            collective_id=0, has_side_effects=True, vmem_limit_bytes=60 << 20
        ),
    )(
        imp_emb.reshape(chunk, BLOCK, D),
        imp_cost.astype(f32).reshape(chunk, LANES),
        camp_emb,
        prices.astype(f32).reshape(1, LANES),
        spend_limits.reshape(1, LANES),
        block_lists.reshape(n_t, -1),
        block_counts,
    )
    return new_prices.reshape(-1), logz.reshape(-1)


def rows_of_chips(mesh):
    n_imp = mesh.shape["imp"]
    coords = [getattr(device, "coords", None) for device in mesh.devices[:, 0]]
    if any(place is None for place in coords):
        return 2 if n_imp % 2 == 0 else 1
    return len({place[1] for place in coords})


def solution(mesh):
    return jax.shard_map(
        functools.partial(local, rows_of_chips(mesh)),
        mesh=mesh,
        in_specs=(
            P(("imp", "camp"), None),
            P(("imp", "camp")),
            P(("camp", "imp"), None),
            P(("camp", "imp")),
            P(("camp", "imp")),
            P("imp", "camp", None),
            P("imp", "camp"),
        ),
        out_specs=(P(("camp", "imp")), P("imp")),
        check_vma=False,
    )
```

```python
import functools

import jax
import jax.numpy as jnp
from jax import lax
from jax.experimental import pallas as pl
from jax.experimental.pallas import tpu as pltpu
from jax.sharding import PartitionSpec as P

D = 256
BLOCK = 128
LANES = 128
STORE_LIMIT = 24 << 20
MESH = pl.DeviceIdType.MESH


def flip(index, bits, size):
    if size & (size - 1):
        return lax.rem(index + bits, size)
    out, bit = index, 1
    while bit < size:
        if bits & bit:
            out = out + bit * (1 - 2 * lax.rem(index // bit, 2))
        bit *= 2
    return out


def unflip(index, bits, size):
    if size & (size - 1):
        return lax.rem(index + size - bits, size)
    return flip(index, bits, size)


def kernel(
    sizes, emb_ref, cost_ref, camp_ref, price_ref, limit_ref, list_ref, count_ref,
    new_ref, logz_ref,
    e_buf, cost_buf, c_buf, price_buf, p_wide, x_buf, m_buf, s_buf, live_buf, f_buf,
    stat_send, stat_recv, spend_send, spend_recv, cost_raw, price_raw, turn_buf, list_buf,
    count_buf, limit_buf,
    local_sem, e_send, e_fwd, e_recv, c_send, c_fwd, c_recv, cost_send, cost_recv,
    price_send, price_recv, stat_ssem, stat_rsem, spend_ssem, spend_rsem,
):
    n_imp, n_camp, n_y, chunk = sizes
    n_z, n_x = n_imp // n_y, n_camp // 2
    n_b = n_imp
    n_t = n_camp * chunk
    stored = x_buf.shape[0] == n_b
    me_i, me_c = lax.axis_index("imp"), lax.axis_index("camp")
    z, y = me_i // n_y, lax.rem(me_i, n_y)
    x, k = me_c // 2, lax.rem(me_c, 2)
    partner = 2 * x + (1 - k)
    scale = 3.0 / jnp.sqrt(jnp.float32(D))

    imp_peers = [
        flip(z, dz, n_z) * n_y + flip(y, dy, n_y)
        for dz in range(n_z) for dy in range(n_y) if dz or dy
    ]
    camp_peers = [partner] + [
        2 * flip(x, dx, n_x) + kk for dx in range(1, n_x) for kk in (k, 1 - k)
    ]

    own_copies = [
        pltpu.make_async_copy(camp_ref, c_buf.at[me_i], local_sem.at[0]),
        pltpu.make_async_copy(emb_ref, e_buf.at[pl.ds(me_c * chunk, chunk)], local_sem.at[1]),
    ]
    small_copies = [
        pltpu.make_async_copy(price_ref, price_raw, local_sem.at[2]),
        pltpu.make_async_copy(cost_ref, cost_raw, local_sem.at[3]),
        pltpu.make_async_copy(list_ref, list_buf, local_sem.at[4]),
        pltpu.make_async_copy(count_ref, count_buf, local_sem.at[5]),
        pltpu.make_async_copy(limit_ref, limit_buf, local_sem.at[6]),
    ]
    for copy in small_copies:
        copy.start()
    for copy in own_copies:
        copy.start()

    barrier = pltpu.get_barrier_semaphore()
    for peer in imp_peers:
        pl.semaphore_signal(barrier, inc=1, device_id={"imp": peer, "camp": me_c}, device_id_type=MESH)
    for peer in camp_peers:
        pl.semaphore_signal(barrier, inc=1, device_id={"imp": me_i, "camp": peer}, device_id_type=MESH)

    turn_buf[...] = jnp.full(turn_buf.shape, -1, jnp.int32)
    for copy in small_copies:
        copy.wait()
    slot = lax.broadcasted_iota(jnp.int32, list_buf.shape, 0)
    turn_buf[: list_buf.shape[0], :n_t] = jnp.where(slot < count_buf[...], list_buf[...], -1)
    named = turn_buf[...].T[:n_t]

    def mark(b, carry):
        hit = jnp.max(jnp.where(named == b, 1.0, 0.0), axis=1, keepdims=True)
        live_buf[b] = jnp.broadcast_to(hit, (n_t, LANES))
        return carry

    lax.fori_loop(0, n_b, mark, 0)
    price_buf[me_i] = price_raw[...].astype(jnp.float32).reshape(1, LANES)
    cost_buf[me_c] = cost_raw[...].astype(jnp.float32).reshape(chunk, LANES)
    pl.semaphore_wait(barrier, len(imp_peers) + len(camp_peers))

    sends = []

    def send(src, dst, ssem, rsem, imp, camp):
        copy = pltpu.make_async_remote_copy(
            src_ref=src, dst_ref=dst, send_sem=ssem, recv_sem=rsem,
            device_id={"imp": imp, "camp": camp}, device_id_type=MESH,
        )
        copy.start()
        sends.append(copy)

    def arrived(dst, ssem, rsem):
        pltpu.make_async_remote_copy(
            src_ref=dst, dst_ref=dst, send_sem=ssem, recv_sem=rsem,
            device_id={"imp": me_i, "camp": partner}, device_id_type=MESH,
        ).wait_recv()

    for dy in range(1, n_y):
        send(camp_ref, c_buf.at[me_i], c_send.at[dy - 1], c_recv.at[me_i],
             z * n_y + flip(y, dy, n_y), me_c)
    for dz in range(1, n_z):
        send(camp_ref, c_buf.at[me_i], c_send.at[n_y - 1 + dz - 1], c_recv.at[me_i],
             flip(z, dz, n_z) * n_y + y, me_c)
    for t in range(chunk):
        for dx in range(1, n_x):
            send(emb_ref.at[t], e_buf.at[me_c * chunk + t], e_send.at[dx, t],
                 e_recv.at[me_c * chunk + t], me_i, 2 * flip(x, dx, n_x) + k)
        send(emb_ref.at[t], e_buf.at[me_c * chunk + t], e_send.at[0, t],
             e_recv.at[me_c * chunk + t], me_i, partner)
    for n, peer in enumerate(imp_peers):
        send(price_buf.at[me_i], price_buf.at[me_i], price_send.at[n], price_recv.at[me_i], peer, me_c)
    for n, peer in enumerate(camp_peers):
        send(cost_buf.at[me_c], cost_buf.at[me_c], cost_send.at[n], cost_recv.at[me_c], me_i, peer)

    for copy in own_copies:
        copy.wait()

    def widen(b):
        p_wide[b] = jnp.broadcast_to(price_buf[b], (BLOCK, LANES)).T

    def score(b, first, count):
        wide = e_buf[pl.ds(first, count)].reshape(count * BLOCK, D)
        raw = lax.dot_general(
            c_buf[b], wide, (((1,), (1,)), ((), ())), preferred_element_type=jnp.float32
        )
        return raw

    def both(b, first, count):
        raw = score(b, first, count)
        for t in range(count):
            logit = raw[:, t * LANES:(t + 1) * LANES] * scale - p_wide[b]
            top = jnp.max(logit, axis=0, keepdims=True)
            expo = jnp.exp(logit - top)
            m_buf[b, pl.ds(first + t, 1), :] = top
            s_buf[b, pl.ds(first + t, 1), :] = jnp.sum(expo, axis=0, keepdims=True)
            if stored:
                x_buf[b, first + t] = expo

    def near(b):
        def step(h, carry):
            both(b, 2 * x * chunk + h * chunk, chunk)
            return carry

        lax.fori_loop(0, 2, step, 0)

    def block_in(b):
        arrived(price_buf.at[b], price_send.at[0], price_recv.at[b])
        widen(b)

    def rows_in(dx, t):
        other = flip(x, dx, n_x)
        tile = (2 * other + k) * chunk + t
        arrived(e_buf.at[tile], e_send.at[0, 0], e_recv.at[tile])
        send(e_buf.at[tile], e_buf.at[tile], e_fwd.at[dx, t], e_recv.at[tile], me_i, partner)

    def rows_there(g):
        for t in range(chunk):
            tile = g * chunk + t
            arrived(e_buf.at[tile], e_send.at[0, 0], e_recv.at[tile])

    widen(me_i)
    rows_there(partner)
    near(me_i)

    order = [(0, dy) for dy in range(1, n_y)] + [(dz, 0) for dz in range(1, n_z)]
    order += [(dz, dy) for dz in range(1, n_z) for dy in range(1, n_y)]
    chunks = [(dx, t) for t in range(chunk) for dx in range(1, n_x)]
    small = n_b * (n_x - 1) <= 8
    seen, groups = [me_i], []
    for n, (dz, dy) in enumerate(order):
        b = flip(z, dz, n_z) * n_y + flip(y, dy, n_y)
        arrived(c_buf.at[b], c_send.at[0], c_recv.at[b])
        if dy == 0:
            for fy in range(1, n_y):
                send(c_buf.at[b], c_buf.at[b], c_fwd.at[dz, fy], c_recv.at[b],
                     z * n_y + flip(y, fy, n_y), me_c)
        block_in(b)
        near(b)
        for g in groups:
            both(b, g * chunk, chunk)
        seen.append(b)
        if chunks and n < len(order) - 1:
            rows_in(*chunks.pop(0))
        if small and not chunks and len(groups) < 2 * (n_x - 1) and n < len(order) - 1:
            dx, own = 1 + len(groups) // 2, len(groups) % 2 == 0
            if own or n == len(order) - 2:
                g = 2 * flip(x, dx, n_x) + (k if own else 1 - k)
                if not own:
                    rows_there(g)
                groups.append(g)
                for early in seen:
                    both(early, g * chunk, chunk)
    while chunks:
        rows_in(*chunks.pop(0))

    for dx in range(1, n_x):
        for kk in (k, 1 - k):
            g = 2 * flip(x, dx, n_x) + kk
            if small and 2 * (dx - 1) + (0 if kk is k else 1) < len(groups):
                continue
            if kk is not k:
                rows_there(g)

            def far(b, carry, g=g):
                both(b, g * chunk, chunk)
                return carry

            lax.fori_loop(0, n_b, far, 0)

    def block_top(b):
        return jnp.where(live_buf[b] > 0.0, m_buf[b], -jnp.inf)

    top_here = lax.fori_loop(
        0, n_b, lambda b, top: jnp.maximum(top, block_top(b)),
        jnp.full((n_t, LANES), -jnp.inf, jnp.float32),
    )
    total_here = lax.fori_loop(
        0, n_b, lambda b, total: total + s_buf[b] * jnp.exp(block_top(b) - top_here),
        jnp.zeros((n_t, LANES), jnp.float32),
    )
    stat_send[0] = top_here
    stat_send[1] = total_here
    for n, peer in enumerate(camp_peers):
        send(stat_send, stat_recv.at[me_c], stat_ssem.at[n], stat_rsem.at[me_c], me_i, peer)
    for peer in camp_peers:
        arrived(cost_buf.at[peer], cost_send.at[0], cost_recv.at[peer])
    cost = jnp.concatenate([cost_buf[g] for g in range(n_camp)], axis=0)
    stat_recv[me_c] = stat_send[...]
    for peer in camp_peers:
        arrived(stat_recv.at[peer], stat_ssem.at[0], stat_rsem.at[peer])
    top = stat_recv[0, 0]
    for g in range(1, n_camp):
        top = jnp.maximum(top, stat_recv[g, 0])
    total = jnp.zeros_like(top)
    for g in range(n_camp):
        total = total + stat_recv[g, 1] * jnp.exp(stat_recv[g, 0] - top)
    logz_ref[...] = top + jnp.log(total)
    ratio = cost / total

    def factor(b, carry):
        f_buf[b] = ratio * jnp.exp(block_top(b) - top)
        return carry

    lax.fori_loop(0, n_b, factor, 0)

    def spend_of(b):
        def step(h, acc):
            first = h * chunk
            if not stored:
                raw = score(b, first, chunk)
            for t in range(chunk):
                if stored:
                    expo = x_buf[b, first + t]
                else:
                    logit = raw[:, t * LANES:(t + 1) * LANES] * scale - p_wide[b]
                    expo = jnp.exp(logit - m_buf[b, pl.ds(first + t, 1), :])
                acc = acc + expo * f_buf[b, pl.ds(first + t, 1), :]
            return acc

        acc = lax.fori_loop(0, n_camp, step, jnp.zeros((BLOCK, LANES), jnp.float32))
        return jnp.sum(acc.T, axis=0, keepdims=True)

    for n, peer in enumerate(reversed(imp_peers)):
        spend_send[peer] = spend_of(peer)
        send(spend_send.at[peer], spend_recv.at[me_i], spend_ssem.at[n], spend_rsem.at[me_i],
             peer, me_c)
    mine = spend_of(me_i)
    for peer in imp_peers:
        arrived(spend_recv.at[peer], spend_ssem.at[0], spend_rsem.at[peer])
        mine = mine + spend_recv[peer]
    limit = limit_buf[...]
    new_ref[...] = price_buf[me_i] + 2.0 * (mine - limit) / (mine + limit)
    for copy in sends:
        copy.wait_send()


def local(n_y, imp_emb, imp_cost, camp_emb, prices, spend_limits, block_lists, block_counts):
    n_imp, n_camp = lax.axis_size("imp"), lax.axis_size("camp")
    chunk = imp_emb.shape[0] // BLOCK
    n_t = n_camp * chunk
    n_b = n_imp
    n_z = n_imp // n_y
    n_x = n_camp // 2
    slots = block_lists.shape[2]
    f32, bf16 = jnp.float32, jnp.bfloat16
    stored = n_b * n_t * BLOCK * LANES * 4 <= STORE_LIMIT
    dma = pltpu.SemaphoreType.DMA
    anywhere, vmem = pl.BlockSpec(memory_space=pl.ANY), pl.BlockSpec(memory_space=pltpu.VMEM)
    new_prices, logz = pl.pallas_call(
        functools.partial(kernel, (n_imp, n_camp, n_y, chunk)),
        out_shape=(
            jax.ShapeDtypeStruct((1, LANES), f32),
            jax.ShapeDtypeStruct((n_t, LANES), f32),
        ),
        in_specs=[anywhere] * 7,
        out_specs=(vmem, vmem),
        scratch_shapes=[
            pltpu.VMEM((n_t, BLOCK, D), bf16),
            pltpu.VMEM((n_camp, chunk, LANES), f32),
            pltpu.VMEM((n_b, BLOCK, D), bf16),
            pltpu.VMEM((n_b, 1, LANES), f32),
            pltpu.VMEM((n_b, BLOCK, LANES), f32),
            pltpu.VMEM((n_b, n_t, BLOCK, LANES) if stored else (1, 1, 8, LANES), f32),
            pltpu.VMEM((n_b, n_t, LANES), f32),
            pltpu.VMEM((n_b, n_t, LANES), f32),
            pltpu.VMEM((n_b, n_t, LANES), f32),
            pltpu.VMEM((n_b, n_t, LANES), f32),
            pltpu.VMEM((2, n_t, LANES), f32),
            pltpu.VMEM((n_camp, 2, n_t, LANES), f32),
            pltpu.VMEM((n_b, 1, LANES), f32),
            pltpu.VMEM((n_b, 1, LANES), f32),
            pltpu.VMEM((chunk * LANES,), bf16),
            pltpu.VMEM((LANES,), bf16),
            pltpu.VMEM((LANES, LANES), jnp.int32),
            pltpu.VMEM((slots, n_t), jnp.int32),
            pltpu.VMEM((1, n_t), jnp.int32),
            pltpu.VMEM((1, LANES), f32),
            dma((7,)),
            dma((n_x, chunk)),
            dma((n_x, chunk)),
            dma((n_t,)),
            dma((n_y + n_z,)),
            dma((n_z, n_y)),
            dma((n_b,)),
            dma((n_camp,)),
            dma((n_camp,)),
            dma((n_imp,)),
            dma((n_imp,)),
            dma((n_camp,)),
            dma((n_camp,)),
            dma((n_imp,)),
            dma((n_imp,)),
        ],
        compiler_params=pltpu.CompilerParams(
            collective_id=0, has_side_effects=True, vmem_limit_bytes=60 << 20
        ),
    )(
        imp_emb.reshape(chunk, BLOCK, D),
        imp_cost,
        camp_emb,
        prices,
        spend_limits.reshape(1, LANES),
        block_lists.transpose(1, 2, 0).reshape(slots, n_t),
        block_counts.T,
    )
    return new_prices.reshape(-1), logz.reshape(-1)


def rows_of_chips(mesh):
    n_imp = mesh.shape["imp"]
    coords = [getattr(device, "coords", None) for device in mesh.devices[:, 0]]
    if any(place is None for place in coords):
        return 2 if n_imp % 2 == 0 else 1
    return len({place[1] for place in coords})


def solution(mesh):
    return jax.shard_map(
        functools.partial(local, rows_of_chips(mesh)),
        mesh=mesh,
        in_specs=(
            P(("imp", "camp"), None),
            P(("imp", "camp")),
            P(("camp", "imp"), None),
            P(("camp", "imp")),
            P(("camp", "imp")),
            P("imp", "camp", None),
            P("imp", "camp"),
        ),
        out_specs=(P(("camp", "imp")), P("imp")),
        check_vma=False,
    )
```

```python
import functools

import jax
import jax.numpy as jnp
from jax import lax
from jax.experimental import pallas as pl
from jax.experimental.pallas import tpu as pltpu
from jax.sharding import PartitionSpec as P

D = 256
BLOCK = 128
LANES = 128
STORE_LIMIT = 24 << 20
MESH = pl.DeviceIdType.MESH


def flip(index, bits, size):
    if size & (size - 1):
        return lax.rem(index + bits, size)
    out, bit = index, 1
    while bit < size:
        if bits & bit:
            out = out + bit * (1 - 2 * lax.rem(index // bit, 2))
        bit *= 2
    return out


def unflip(index, bits, size):
    if size & (size - 1):
        return lax.rem(index + size - bits, size)
    return flip(index, bits, size)


def kernel(
    sizes, emb_ref, cost_ref, camp_ref, price_ref, limit_ref, list_ref, count_ref,
    new_ref, logz_ref,
    e_buf, cost_buf, c_buf, price_buf, p_wide, x_buf, m_buf, s_buf, live_buf, f_buf,
    stat_send, stat_recv, spend_send, spend_recv, cost_raw, price_raw, turn_buf, list_buf,
    count_buf, limit_buf,
    local_sem, e_send, e_fwd, e_recv, c_send, c_fwd, c_recv, cost_send, cost_recv,
    price_send, price_recv, stat_ssem, stat_rsem, spend_ssem, spend_rsem,
):
    n_imp, n_camp, n_y, chunk = sizes
    n_z, n_x = n_imp // n_y, n_camp // 2
    n_b = n_imp
    n_t = n_camp * chunk
    stored = x_buf.shape[0] == n_b
    me_i, me_c = lax.axis_index("imp"), lax.axis_index("camp")
    z, y = me_i // n_y, lax.rem(me_i, n_y)
    x, k = me_c // 2, lax.rem(me_c, 2)
    partner = 2 * x + (1 - k)
    scale = 3.0 / jnp.sqrt(jnp.float32(D))

    imp_peers = [
        flip(z, dz, n_z) * n_y + flip(y, dy, n_y)
        for dz in range(n_z) for dy in range(n_y) if dz or dy
    ]
    camp_peers = [partner] + [
        2 * flip(x, dx, n_x) + kk for dx in range(1, n_x) for kk in (k, 1 - k)
    ]

    own_copies = [
        pltpu.make_async_copy(camp_ref, c_buf.at[me_i], local_sem.at[0]),
        pltpu.make_async_copy(emb_ref, e_buf.at[pl.ds(me_c * chunk, chunk)], local_sem.at[1]),
    ]
    small_copies = [
        pltpu.make_async_copy(price_ref, price_raw, local_sem.at[2]),
        pltpu.make_async_copy(cost_ref, cost_raw, local_sem.at[3]),
        pltpu.make_async_copy(list_ref, list_buf, local_sem.at[4]),
        pltpu.make_async_copy(count_ref, count_buf, local_sem.at[5]),
        pltpu.make_async_copy(limit_ref, limit_buf, local_sem.at[6]),
    ]
    for copy in small_copies:
        copy.start()
    for copy in own_copies:
        copy.start()

    barrier = pltpu.get_barrier_semaphore()
    for peer in imp_peers:
        pl.semaphore_signal(barrier, inc=1, device_id={"imp": peer, "camp": me_c}, device_id_type=MESH)
    for peer in camp_peers:
        pl.semaphore_signal(barrier, inc=1, device_id={"imp": me_i, "camp": peer}, device_id_type=MESH)

    turn_buf[...] = jnp.full(turn_buf.shape, -1, jnp.int32)
    for copy in small_copies:
        copy.wait()
    slot = lax.broadcasted_iota(jnp.int32, list_buf.shape, 0)
    turn_buf[: list_buf.shape[0], :n_t] = jnp.where(slot < count_buf[...], list_buf[...], -1)
    named = turn_buf[...].T[:n_t]

    def mark(b, carry):
        hit = jnp.max(jnp.where(named == b, 1.0, 0.0), axis=1, keepdims=True)
        live_buf[b] = jnp.broadcast_to(hit, (n_t, LANES))
        return carry

    lax.fori_loop(0, n_b, mark, 0, unroll=n_b <= 8)
    price_buf[me_i] = price_raw[...].astype(jnp.float32).reshape(1, LANES)
    cost_buf[me_c] = cost_raw[...].astype(jnp.float32).reshape(chunk, LANES)
    pl.semaphore_wait(barrier, len(imp_peers) + len(camp_peers))

    sends = []

    def send(src, dst, ssem, rsem, imp, camp):
        copy = pltpu.make_async_remote_copy(
            src_ref=src, dst_ref=dst, send_sem=ssem, recv_sem=rsem,
            device_id={"imp": imp, "camp": camp}, device_id_type=MESH,
        )
        copy.start()
        sends.append(copy)

    def arrived(dst, ssem, rsem):
        pltpu.make_async_remote_copy(
            src_ref=dst, dst_ref=dst, send_sem=ssem, recv_sem=rsem,
            device_id={"imp": me_i, "camp": partner}, device_id_type=MESH,
        ).wait_recv()

    for dy in range(1, n_y):
        send(camp_ref, c_buf.at[me_i], c_send.at[dy - 1], c_recv.at[me_i],
             z * n_y + flip(y, dy, n_y), me_c)
    for dz in range(1, n_z):
        send(camp_ref, c_buf.at[me_i], c_send.at[n_y - 1 + dz - 1], c_recv.at[me_i],
             flip(z, dz, n_z) * n_y + y, me_c)
    for t in range(chunk):
        for dx in range(1, n_x):
            send(emb_ref.at[t], e_buf.at[me_c * chunk + t], e_send.at[dx, t],
                 e_recv.at[me_c * chunk + t], me_i, 2 * flip(x, dx, n_x) + k)
        send(emb_ref.at[t], e_buf.at[me_c * chunk + t], e_send.at[0, t],
             e_recv.at[me_c * chunk + t], me_i, partner)
    for n, peer in enumerate(imp_peers):
        send(price_buf.at[me_i], price_buf.at[me_i], price_send.at[n], price_recv.at[me_i], peer, me_c)
    for n, peer in enumerate(camp_peers):
        send(cost_buf.at[me_c], cost_buf.at[me_c], cost_send.at[n], cost_recv.at[me_c], me_i, peer)

    for copy in own_copies:
        copy.wait()

    def widen(b):
        p_wide[b] = jnp.broadcast_to(price_buf[b], (BLOCK, LANES)).T

    def score(b, first, count):
        wide = e_buf[pl.ds(first, count)].reshape(count * BLOCK, D)
        raw = lax.dot_general(
            c_buf[b], wide, (((1,), (1,)), ((), ())), preferred_element_type=jnp.float32
        )
        return raw

    def both(b, first, count):
        raw = score(b, first, count)
        for t in range(count):
            logit = raw[:, t * LANES:(t + 1) * LANES] * scale - p_wide[b]
            top = jnp.max(logit, axis=0, keepdims=True)
            expo = jnp.exp(logit - top)
            m_buf[b, pl.ds(first + t, 1), :] = top
            s_buf[b, pl.ds(first + t, 1), :] = jnp.sum(expo, axis=0, keepdims=True)
            if stored:
                x_buf[b, first + t] = expo

    def near(b):
        def step(h, carry):
            both(b, 2 * x * chunk + h * chunk, chunk)
            return carry

        lax.fori_loop(0, 2, step, 0)

    def block_in(b):
        arrived(price_buf.at[b], price_send.at[0], price_recv.at[b])
        widen(b)

    def rows_in(dx, t):
        other = flip(x, dx, n_x)
        tile = (2 * other + k) * chunk + t
        arrived(e_buf.at[tile], e_send.at[0, 0], e_recv.at[tile])
        send(e_buf.at[tile], e_buf.at[tile], e_fwd.at[dx, t], e_recv.at[tile], me_i, partner)

    def rows_there(g):
        for t in range(chunk):
            tile = g * chunk + t
            arrived(e_buf.at[tile], e_send.at[0, 0], e_recv.at[tile])

    widen(me_i)
    rows_there(partner)
    near(me_i)

    order = [(0, dy) for dy in range(1, n_y)] + [(dz, 0) for dz in range(1, n_z)]
    order += [(dz, dy) for dz in range(1, n_z) for dy in range(1, n_y)]
    chunks = [(dx, t) for t in range(chunk) for dx in range(1, n_x)]
    small = n_b * (n_x - 1) <= 8
    seen, groups = [me_i], []
    for n, (dz, dy) in enumerate(order):
        b = flip(z, dz, n_z) * n_y + flip(y, dy, n_y)
        arrived(c_buf.at[b], c_send.at[0], c_recv.at[b])
        if dy == 0:
            for fy in range(1, n_y):
                send(c_buf.at[b], c_buf.at[b], c_fwd.at[dz, fy], c_recv.at[b],
                     z * n_y + flip(y, fy, n_y), me_c)
        block_in(b)
        near(b)
        for g in groups:
            both(b, g * chunk, chunk)
        seen.append(b)
        if chunks and n < len(order) - 1:
            rows_in(*chunks.pop(0))
        if small and not chunks and len(groups) < 2 * (n_x - 1) and n < len(order) - 1:
            dx, own = 1 + len(groups) // 2, len(groups) % 2 == 0
            if own or n == len(order) - 2:
                g = 2 * flip(x, dx, n_x) + (k if own else 1 - k)
                if not own:
                    rows_there(g)
                groups.append(g)
                for early in seen:
                    both(early, g * chunk, chunk)
    while chunks:
        rows_in(*chunks.pop(0))

    for dx in range(1, n_x):
        for kk in (k, 1 - k):
            g = 2 * flip(x, dx, n_x) + kk
            if small and 2 * (dx - 1) + (0 if kk is k else 1) < len(groups):
                continue
            if kk is not k:
                rows_there(g)

            def far(b, carry, g=g):
                both(b, g * chunk, chunk)
                return carry

            lax.fori_loop(0, n_b, far, 0)

    def block_top(b):
        return jnp.where(live_buf[b] > 0.0, m_buf[b], -jnp.inf)

    top_here = lax.fori_loop(
        0, n_b, lambda b, top: jnp.maximum(top, block_top(b)),
        jnp.full((n_t, LANES), -jnp.inf, jnp.float32), unroll=n_b <= 8,
    )
    total_here = lax.fori_loop(
        0, n_b, lambda b, total: total + s_buf[b] * jnp.exp(block_top(b) - top_here),
        jnp.zeros((n_t, LANES), jnp.float32), unroll=n_b <= 8,
    )
    stat_send[0] = top_here
    stat_send[1] = total_here
    for n, peer in enumerate(camp_peers):
        send(stat_send, stat_recv.at[me_c], stat_ssem.at[n], stat_rsem.at[me_c], me_i, peer)
    for peer in camp_peers:
        arrived(cost_buf.at[peer], cost_send.at[0], cost_recv.at[peer])
    cost = jnp.concatenate([cost_buf[g] for g in range(n_camp)], axis=0)
    stat_recv[me_c] = stat_send[...]
    for peer in camp_peers:
        arrived(stat_recv.at[peer], stat_ssem.at[0], stat_rsem.at[peer])
    top = stat_recv[0, 0]
    for g in range(1, n_camp):
        top = jnp.maximum(top, stat_recv[g, 0])
    total = jnp.zeros_like(top)
    for g in range(n_camp):
        total = total + stat_recv[g, 1] * jnp.exp(stat_recv[g, 0] - top)
    logz_ref[...] = top + jnp.log(total)
    ratio = cost / total

    def factor(b, carry):
        f_buf[b] = ratio * jnp.exp(block_top(b) - top)
        return carry

    lax.fori_loop(0, n_b, factor, 0, unroll=n_b <= 8)

    def spend_of(b):
        def step(h, acc):
            first = h * chunk
            if not stored:
                raw = score(b, first, chunk)
            for t in range(chunk):
                if stored:
                    expo = x_buf[b, first + t]
                else:
                    logit = raw[:, t * LANES:(t + 1) * LANES] * scale - p_wide[b]
                    expo = jnp.exp(logit - m_buf[b, pl.ds(first + t, 1), :])
                acc = acc + expo * f_buf[b, pl.ds(first + t, 1), :]
            return acc

        acc = lax.fori_loop(0, n_camp, step, jnp.zeros((BLOCK, LANES), jnp.float32))
        return jnp.sum(acc.T, axis=0, keepdims=True)

    for n, peer in enumerate(reversed(imp_peers)):
        spend_send[peer] = spend_of(peer)
        send(spend_send.at[peer], spend_recv.at[me_i], spend_ssem.at[n], spend_rsem.at[me_i],
             peer, me_c)
    mine = spend_of(me_i)
    for peer in imp_peers:
        arrived(spend_recv.at[peer], spend_ssem.at[0], spend_rsem.at[peer])
        mine = mine + spend_recv[peer]
    limit = limit_buf[...]
    new_ref[...] = price_buf[me_i] + 2.0 * (mine - limit) / (mine + limit)
    for copy in sends:
        copy.wait_send()


def local(n_y, imp_emb, imp_cost, camp_emb, prices, spend_limits, block_lists, block_counts):
    n_imp, n_camp = lax.axis_size("imp"), lax.axis_size("camp")
    chunk = imp_emb.shape[0] // BLOCK
    n_t = n_camp * chunk
    n_b = n_imp
    n_z = n_imp // n_y
    n_x = n_camp // 2
    slots = block_lists.shape[2]
    f32, bf16 = jnp.float32, jnp.bfloat16
    stored = n_b * n_t * BLOCK * LANES * 4 <= STORE_LIMIT
    dma = pltpu.SemaphoreType.DMA
    anywhere, vmem = pl.BlockSpec(memory_space=pl.ANY), pl.BlockSpec(memory_space=pltpu.VMEM)
    new_prices, logz = pl.pallas_call(
        functools.partial(kernel, (n_imp, n_camp, n_y, chunk)),
        out_shape=(
            jax.ShapeDtypeStruct((1, LANES), f32),
            jax.ShapeDtypeStruct((n_t, LANES), f32),
        ),
        in_specs=[anywhere] * 7,
        out_specs=(vmem, vmem),
        scratch_shapes=[
            pltpu.VMEM((n_t, BLOCK, D), bf16),
            pltpu.VMEM((n_camp, chunk, LANES), f32),
            pltpu.VMEM((n_b, BLOCK, D), bf16),
            pltpu.VMEM((n_b, 1, LANES), f32),
            pltpu.VMEM((n_b, BLOCK, LANES), f32),
            pltpu.VMEM((n_b, n_t, BLOCK, LANES) if stored else (1, 1, 8, LANES), f32),
            pltpu.VMEM((n_b, n_t, LANES), f32),
            pltpu.VMEM((n_b, n_t, LANES), f32),
            pltpu.VMEM((n_b, n_t, LANES), f32),
            pltpu.VMEM((n_b, n_t, LANES), f32),
            pltpu.VMEM((2, n_t, LANES), f32),
            pltpu.VMEM((n_camp, 2, n_t, LANES), f32),
            pltpu.VMEM((n_b, 1, LANES), f32),
            pltpu.VMEM((n_b, 1, LANES), f32),
            pltpu.VMEM((chunk * LANES,), bf16),
            pltpu.VMEM((LANES,), bf16),
            pltpu.VMEM((LANES, LANES), jnp.int32),
            pltpu.VMEM((slots, n_t), jnp.int32),
            pltpu.VMEM((1, n_t), jnp.int32),
            pltpu.VMEM((1, LANES), f32),
            dma((7,)),
            dma((n_x, chunk)),
            dma((n_x, chunk)),
            dma((n_t,)),
            dma((n_y + n_z,)),
            dma((n_z, n_y)),
            dma((n_b,)),
            dma((n_camp,)),
            dma((n_camp,)),
            dma((n_imp,)),
            dma((n_imp,)),
            dma((n_camp,)),
            dma((n_camp,)),
            dma((n_imp,)),
            dma((n_imp,)),
        ],
        compiler_params=pltpu.CompilerParams(
            collective_id=0, has_side_effects=True, vmem_limit_bytes=60 << 20
        ),
    )(
        imp_emb.reshape(chunk, BLOCK, D),
        imp_cost,
        camp_emb,
        prices,
        spend_limits.reshape(1, LANES),
        block_lists.transpose(1, 2, 0).reshape(slots, n_t),
        block_counts.T,
    )

    def hand(a_ref, b_ref, c_ref, d_ref):
        c_ref[...] = a_ref[...]
        d_ref[...] = b_ref[...]

    new_prices, logz = pl.pallas_call(
        hand,
        out_shape=(
            jax.ShapeDtypeStruct((1, LANES), f32),
            jax.ShapeDtypeStruct((n_t, LANES), f32),
        ),
        in_specs=[vmem] * 2,
        out_specs=(vmem, vmem),
    )(new_prices, logz)
    return new_prices.reshape(-1), logz.reshape(-1)


def rows_of_chips(mesh):
    n_imp = mesh.shape["imp"]
    coords = [getattr(device, "coords", None) for device in mesh.devices[:, 0]]
    if any(place is None for place in coords):
        return 2 if n_imp % 2 == 0 else 1
    return len({place[1] for place in coords})


def solution(mesh):
    return jax.shard_map(
        functools.partial(local, rows_of_chips(mesh)),
        mesh=mesh,
        in_specs=(
            P(("imp", "camp"), None),
            P(("imp", "camp")),
            P(("camp", "imp"), None),
            P(("camp", "imp")),
            P(("camp", "imp")),
            P("imp", "camp", None),
            P("imp", "camp"),
        ),
        out_specs=(P(("camp", "imp")), P("imp")),
        check_vma=False,
    )
```
